1024 devices in a mesh: ctx: 16 (over x, z_hi), tp: 16 (over z_lo, core), grp: 4 (over y).
Axes of the slice: x: 4, y: 4, z: 32 (z_hi: 4, z_lo: 8; z = z_hi * 8 + z_lo), core: 2. Of those that a mesh axis runs over, the one named last changes fastest.
Arguments:
- pre_act: bfloat16 [16384, 5120], P(('ctx', 'grp')), may hold values from -6 to 6
- w_out: bfloat16 [5120, 8192], P(None, 'tp'), may hold values from -0.078125 to 0.078125
- b_out: bfloat16 [8192], P('tp'), may hold values from -3 to 3
- row_slot: int32 [16384], P(('ctx', 'grp')), may hold values from 0 to 511, as said below
- ctx_slot: int32 [32768], P(('ctx', 'grp')), may hold values from -1 to 511, as said below
- text_rows: bfloat16 [32768, 8192], P(('ctx', 'grp'), 'tp'), may hold values from -6 to 6
- cotangent: bfloat16 [32768, 8192], P(('ctx', 'grp'), 'tp'), may hold values from -6 to 6
Outputs:
- embeds: bfloat16 [32768, 8192], P(('ctx', 'grp'), 'tp')
- grad_pre: bfloat16 [16384, 5120], P(('ctx', 'grp'))
The draws below stay inside these ranges and needn't reach their ends.
Inputs may be any that keep to these rules, and one draw needn't show every extreme that they name: `row_slot`: within each aligned block of 256 rows (one encoder device) the values are distinct; value // 8 is the context shard (index along ctx+grp) that receives the row and value % 8 its slot there; in every block some shard receives exactly 8 rows. `ctx_slot`: within each aligned block of 512 positions (one context shard) the values other than -1 are distinct; a value s names the row that encoder device s // 8 (index along ctx+grp) sent in slot s % 8 to this shard; every image token is placed at exactly one position and every used slot names a sent row.
All inputs are finite; a program needn't handle non-finite values.
Results may differ from the reference program's by a relative error of at most 0.018.
Values may be sent and summed in bfloat16 or wider, within the bound.
A program may use at most 64 MiB of HBM per device.

```python
import jax
import jax.numpy as jnp
from jax import lax

D = 8192
D_IN = 5120
ROWS_DEV = 256
TOK_DEV = 512
CAP = 8
IMAGES = 16384
CONTEXT = 32768
N_CTX = 16
N_TP = 16
N_GRP = 4


def routing_tables(key):
    groups = N_CTX * N_GRP
    slot_count = groups * CAP
    base = jax.random.fold_in(key, 9173)
    key_hot, key_noise, key_rows, key_places = jax.random.split(base, 4)
    hot_shard = jax.random.randint(key_hot, (groups,), 0, groups)
    random_part = jax.random.randint(key_noise, (groups, slot_count), 0, 65536)
    slot_ids = jnp.arange(slot_count, dtype=jnp.int32)
    is_hot = slot_ids[None, :] // CAP == hot_shard[:, None]
    forced = (jnp.arange(groups, dtype=jnp.int32)[:, None] == 0) & ((slot_ids[None, :] == 0) | (slot_ids[None, :] == slot_count - 1))
    scores = random_part * slot_count + slot_ids[None, :] + (is_hot | forced).astype(jnp.int32) * (65536 * slot_count)
    ranking = jnp.argsort(-scores, axis=1)
    chosen = ranking[:, :ROWS_DEV].astype(jnp.int32)
    row_noise = jax.random.randint(key_rows, (groups, ROWS_DEV), 0, 65536) * ROWS_DEV + jnp.arange(ROWS_DEV, dtype=jnp.int32)[None, :]
    shuffle = jnp.argsort(row_noise, axis=1)
    chosen = jnp.take_along_axis(chosen, shuffle, axis=1)
    row_slot = chosen.reshape(-1)
    in_use = jnp.zeros((groups, slot_count), jnp.int32).at[jnp.arange(groups, dtype=jnp.int32)[:, None], chosen].set(1)
    received = in_use.reshape(groups, groups, CAP).transpose(1, 0, 2).reshape(groups, slot_count)
    listing = jnp.argsort((1 - received) * slot_count + slot_ids[None, :], axis=1).astype(jnp.int32)
    counts = jnp.sum(received, axis=1)
    place_noise = jax.random.randint(key_places, (groups, TOK_DEV), 0, 65536) * TOK_DEV + jnp.arange(TOK_DEV, dtype=jnp.int32)[None, :]
    positions = jnp.argsort(place_noise, axis=1)[:, :slot_count]
    values = jnp.where(slot_ids[None, :] < counts[:, None], listing, -1)
    ctx_table = jnp.full((groups, TOK_DEV), -1, jnp.int32).at[jnp.arange(groups, dtype=jnp.int32)[:, None], positions].set(values)
    return (row_slot, ctx_table.reshape(-1))


def draw_row_slot(key, part):
    return routing_tables(key)[0]


def draw_ctx_slot(key, part):
    return routing_tables(key)[1]


def levels(rng, extent, shards, low, largest):
    def one(position, parts):
        heights = jax.random.uniform(jax.random.fold_in(jax.random.fold_in(rng, 6), position), (parts,), jnp.float32, low / len(shards), largest / len(shards))
        return jnp.repeat(jnp.exp(heights), extent[position] // parts).reshape((-1,) + (1,) * (len(extent) - position - 1))

    loudness = one(*shards[0])
    for cut in shards[1:]:
        loudness = loudness * one(*cut)
    return loudness


def scatter_about(stream_key, dims, scale, most, cuts=(), held_as=jnp.bfloat16):
    gain = levels(stream_key, dims, cuts, -0.22, 0.18) if cuts else 1.0
    result = jax.random.normal(stream_key, dims, jnp.float32) * scale * gain
    return jnp.minimum(jnp.maximum(result, -most), most).astype(held_as)


def setup_inputs(seed: int = 0) -> dict:
    key_list = jax.random.split(jax.random.key(seed), 8)
    return {
        "pre_act": scatter_about(key_list[0], (IMAGES, D_IN), 1.0, 6.0, ((0, 64),)),
        "w_out": scatter_about(key_list[1], (D_IN, D), D_IN ** -0.5, 0.078125, ((1, 16),)),
        "b_out": scatter_about(key_list[2], (D,), 0.5, 3.0, ((0, 16),)),
        "row_slot": draw_row_slot(jax.random.fold_in(key_list[7], 71), 0),
        "ctx_slot": draw_ctx_slot(jax.random.fold_in(key_list[7], 71), 0),
        "text_rows": scatter_about(key_list[5], (CONTEXT, D), 1.0, 6.0, ((0, 64), (1, 16))),
        "cotangent": scatter_about(key_list[6], (CONTEXT, D), 1.0, 6.0, ((0, 64), (1, 16))),
    }


def gelu_value(values):
    return 0.5 * values * (1.0 + lax.erf(values * 0.7071067811865476))


def gelu_slope(values):
    return 0.5 * (1.0 + lax.erf(values * 0.7071067811865476)) + values * jnp.exp(-0.5 * values * values) * 0.3989422804014327


def reference(pre_act, w_out, b_out, row_slot, ctx_slot, text_rows, cotangent):
    images = pre_act.shape[0]
    slot_count = 2 * ROWS_DEV
    width = D // N_TP
    pre_float = pre_act.astype(jnp.float32)
    hidden = gelu_value(pre_float).astype(jnp.bfloat16)
    merged = (jnp.dot(hidden, w_out, preferred_element_type=jnp.float32) + b_out.astype(jnp.float32)).astype(jnp.bfloat16)
    sender = jnp.arange(images, dtype=jnp.int32) // ROWS_DEV
    target = row_slot // CAP
    landing = target * slot_count + sender * CAP + row_slot % CAP
    lookup = jnp.zeros((N_CTX * N_GRP * slot_count,), jnp.int32).at[landing].set(jnp.arange(images, dtype=jnp.int32))
    shard_of = jnp.arange(ctx_slot.shape[0], dtype=jnp.int32) // TOK_DEV
    placed = ctx_slot >= 0
    row_at = lookup[jnp.where(placed, shard_of * slot_count + ctx_slot, 0)]
    embeds = jnp.where(placed[:, None], merged[row_at], text_rows)
    grad_rows = jnp.zeros((images, D), jnp.bfloat16).at[jnp.where(placed, row_at, images)].set(cotangent, mode="drop")
    summed = jnp.zeros((images, D_IN), jnp.float32)
    for group_index in range(N_TP):
        lower = group_index * width
        term = lax.dot_general(grad_rows[:, lower:lower + width], w_out[:, lower:lower + width], (((1,), (1,)), ((), ())), preferred_element_type=jnp.float32)
        rounded = lax.optimization_barrier(term.astype(jnp.bfloat16))
        summed = summed + rounded.astype(jnp.float32)
    grad_pre = (summed * gelu_slope(pre_float)).astype(jnp.bfloat16)
    return embeds, grad_pre
```

```python
import functools

import jax
import jax.numpy as jnp
from jax import lax
from jax.experimental import pallas as pl
from jax.experimental.pallas import tpu as pltpu
from jax.sharding import Mesh
from jax.sharding import PartitionSpec as P

MESH = pl.DeviceIdType.MESH
CHUNKS = 20
LAG = 3


def gelu_value(values):
    return 0.5 * values * (1.0 + lax.erf(values * 0.7071067811865476))


def gelu_slope(values):
    return (
        0.5 * (1.0 + lax.erf(values * 0.7071067811865476))
        + values * jnp.exp(-0.5 * values * values) * 0.3989422804014327
    )


def remote(src, dst, send, recv, peer):
    return pltpu.make_async_remote_copy(
        src_ref=src, dst_ref=dst, send_sem=send, recv_sem=recv, device_id=peer, device_id_type=MESH
    )


def nt_dot(left, right):
    return lax.dot_general(
        left, right, (((1,), (1,)), ((), ())), preferred_element_type=jnp.float32
    )


def kernel(
    sizes, cap,
    merged, cot, text, w, pre, row_out, tok_out, row_in, tok_in,
    emb, grad,
    out_buf, z_buf, relay, x_buf, y_buf, w_far, rows_full, rows_far, flow_in, flow_out, acc,
    z_send, z_recv, x_send, x_recv, y_send, y_recv,
    w_send, w_recv, g_send, g_recv,
    flow_send, flow_recv, fin_send, fin_recv, mate_send, mate_recv,
):
    nz, nx, ny, nl = sizes
    zh, xx, yy = lax.axis_index("zh"), lax.axis_index("x"), lax.axis_index("y")
    line, core = lax.axis_index("zl"), lax.axis_index("core")
    mate = {"core": 1 - core}
    right, left = {"zh": lax.rem(zh + 1, nz)}, {"zh": lax.rem(zh + nz - 1, nz)}
    up, down = {"zl": line + 1}, {"zl": line - 1}
    x_peer = [{"x": lax.rem(xx + e, nx)} for e in range(nx)]
    y_peer = [{"y": lax.rem(yy + f, ny)} for f in range(ny)]
    blocks = nz * nx * ny
    slots = blocks * 2 * cap
    tokens, width = cot.shape
    half_width = width // 2
    rows = merged.shape[0]
    half_rows = rows // 2
    count, piece = flow_out.shape[0], flow_out.shape[2]
    shape6 = (nz, nx, ny, 2 * cap, half_width)

    middle = nl // 2 - 1 + core if nl > 1 else 0 * core
    has_low = jnp.logical_and(line <= middle, line > 0)
    has_high = jnp.logical_and(line >= middle, line < nl - 1)

    barrier = pltpu.get_barrier_semaphore()
    greeted = [mate] + x_peer[1:] + y_peer[1:]
    if nz > 1:
        greeted += [right, left]
    for peer in greeted:
        pl.semaphore_signal(barrier, inc=1, device_id=peer, device_id_type=MESH)

    @pl.when(line > 0)
    def _():
        pl.semaphore_signal(barrier, inc=1, device_id=down, device_id_type=MESH)

    @pl.when(line < nl - 1)
    def _():
        pl.semaphore_signal(barrier, inc=1, device_id=up, device_id_type=MESH)

    pl.semaphore_wait(
        barrier,
        len(greeted) + (line > 0).astype(jnp.int32) + (line < nl - 1).astype(jnp.int32),
    )

    def place(b, source, where):
        total = jnp.zeros((slots, half_width), jnp.float32)
        ids = lax.broadcasted_iota(jnp.int32, (slots, source.shape[0]), 0)
        for h in range(2):
            hot = (ids == where[...] + h * cap).astype(jnp.bfloat16)
            part = source[:, h * half_width : (h + 1) * half_width]
            total += jnp.dot(hot, part, preferred_element_type=jnp.float32)
        out_buf[b] = total.astype(jnp.bfloat16).reshape(shape6)

    def pick(b, where, h):
        ids = lax.broadcasted_iota(jnp.int32, (where.shape[0], slots), 1)
        hot = (ids == where[...] + h * cap).astype(jnp.bfloat16)
        data = y_buf[b].reshape(slots, half_width)
        return jnp.dot(hot, data, preferred_element_type=jnp.float32)

    cut = nx // 2

    def z_copy(b, n):
        src, dst, peer = (
            lambda: (out_buf.at[b, 2, :cut], relay.at[b, 0], right),
            lambda: (out_buf.at[b, 2, cut:], relay.at[b, 1], left),
            lambda: (out_buf.at[b, 1], z_buf.at[b, 0], right),
            lambda: (out_buf.at[b, 3], z_buf.at[b, 2], left),
            lambda: (relay.at[b, 0], z_buf.at[b, 1, :cut], right),
            lambda: (relay.at[b, 1], z_buf.at[b, 1, cut:], left),
        )[n]()
        return remote(src, dst, z_send.at[b, n], z_recv.at[b, n], peer)

    def x_copy(b, d, e):
        src = out_buf.at[b, 0, e] if d == 0 else z_buf.at[b, d - 1, e]
        dst = x_buf.at[b, d, e]
        if e == 0:
            return pltpu.make_async_copy(src, dst, x_recv.at[b, d, 0])
        return remote(src, dst, x_send.at[b, d, e], x_recv.at[b, d, e], x_peer[e])

    def y_copy(b, d, f):
        src, dst = x_buf.at[b, d, :, f], y_buf.at[b, d, :, f]
        if f == 0:
            return pltpu.make_async_copy(src, dst, y_recv.at[b, d, 0])
        return remote(src, dst, y_send.at[b, d, f], y_recv.at[b, d, f], y_peer[f])

    def z_start(b):
        if nz > 1:
            for n in range(4):
                z_copy(b, n).start()

    def z_forward(b):
        if nz > 1:
            for n in (0, 1):
                z_copy(b, n).wait_recv()
                z_copy(b, n + 4).start()

    def z_arrive(b, d):
        for n in {0: (), 1: (2,), 2: (4, 5), 3: (3,)}[d]:
            z_copy(b, n).wait_recv()

    def x_start(b, d):
        for e in list(range(1, nx)) + [0]:
            x_copy(b, d, e).start()

    def y_start(b, d):
        x_copy(b, d, 0).wait()
        for e in range(1, nx):
            x_copy(b, d, e).wait_recv()
        for f in list(range(1, ny)) + [0]:
            y_copy(b, d, f).start()

    def y_arrive(b, d):
        y_copy(b, d, 0).wait()
        for f in range(1, ny):
            y_copy(b, d, f).wait_recv()

    w_copy = remote(w, w_far, w_send, w_recv, mate)
    w_copy.start()

    place(0, cot, tok_out)
    z_start(0)
    x_start(0, 0)
    place(1, merged, row_out)
    y_start(0, 0)
    z_forward(0)
    z_start(1)
    x_start(1, 0)
    y_start(1, 0)
    far = [1, 3, 2] if nz > 1 else []
    for d in far:
        z_arrive(0, d)
        x_start(0, d)
        y_start(0, d)
    for d in range(nz):
        y_arrive(0, d)

    for h in range(2):
        rows_full[:, h * half_width : (h + 1) * half_width] = pick(0, row_in, h).astype(
            jnp.bfloat16
        )
    mine = pl.ds(pl.multiple_of(core * half_rows, half_rows), half_rows)
    other = pl.ds(pl.multiple_of((1 - core) * half_rows, half_rows), half_rows)
    g_copy = remote(rows_full.at[other], rows_far, g_send, g_recv, mate)
    g_copy.start()
    z_forward(1)
    w_copy.wait_recv()
    g_copy.wait_recv()

    def columns(i):
        return pl.ds(pl.multiple_of(i * piece, piece), piece)

    def flow_copy(i, side, peer):
        return remote(
            flow_out.at[i], flow_in.at[side, i], flow_send.at[i], flow_recv.at[side, i], peer
        )

    def fin_copy(i, side, peer):
        block = grad.at[mine, columns(i)]
        return remote(block, block, fin_send.at[side, i], fin_recv.at[i], peer)

    def mate_copy(i):
        block = grad.at[mine, columns(i)]
        return remote(block, block, mate_send.at[i], mate_recv.at[i], mate)

    def mate_block(i):
        block = grad.at[other, columns(i)]
        return remote(block, block, mate_send.at[i], mate_recv.at[i], mate)

    def publish(i):
        @pl.when(has_low)
        def _():
            fin_copy(i, 0, down).start()

        @pl.when(has_high)
        def _():
            fin_copy(i, 1, up).start()

        mate_copy(i).start()

    away = jnp.where(line < middle, middle - line, line - middle)
    lag = 1 + LAG * away
    steps = count + 1 + LAG * (nl // 2 + (1 if nl > 1 else 0))

    def step(i, carry):
        @pl.when(i < count)
        def _():
            acc[...] = nt_dot(rows_full[mine, :], w[columns(i), :]) + nt_dot(
                rows_far[...], w_far[columns(i), :]
            )

            @pl.when(has_low)
            def _():
                flow_copy(i, 0, up).wait_recv()
                acc[...] += flow_in[0, i].astype(jnp.float32)

            @pl.when(has_high)
            def _():
                flow_copy(i, 1, down).wait_recv()
                acc[...] += flow_in[1, i].astype(jnp.float32)

            @pl.when(line != middle)
            def _():
                flow_out[i] = acc[...].astype(jnp.bfloat16)

            @pl.when(line < middle)
            def _():
                flow_copy(i, 0, up).start()

            @pl.when(line > middle)
            def _():
                flow_copy(i, 1, down).start()

            @pl.when(line == middle)
            def _():
                slope = gelu_slope(pre[mine, columns(i)].astype(jnp.float32))
                grad[mine, columns(i)] = (acc[...] * slope).astype(jnp.bfloat16)
                publish(i)

        j = i - lag

        @pl.when(jnp.logical_and(line != middle, jnp.logical_and(j >= 0, j < count)))
        def _():
            fin_copy(j, 0, down).wait_recv()
            publish(j)

        return carry

    first, second = count // 2, count // 2 + 3
    lax.fori_loop(0, first, step, 0)
    for d in far:
        z_arrive(1, d)
        x_start(1, d)
    lax.fori_loop(first, second, step, 0)
    for d in far:
        y_start(1, d)
    lax.fori_loop(second, steps, step, 0)

    for d in range(nz):
        y_arrive(1, d)
    for h in range(2):
        part = pl.ds(h * half_width, half_width)
        emb[:, part] = jnp.where(
            tok_in[...] >= 0, pick(1, tok_in, h).astype(jnp.bfloat16), text[:, part]
        )

    def drain(i, carry):
        @pl.when(line < middle)
        def _():
            flow_copy(i, 0, up).wait_send()

        @pl.when(line > middle)
        def _():
            flow_copy(i, 1, down).wait_send()

        @pl.when(has_low)
        def _():
            fin_copy(i, 0, down).wait_send()

        @pl.when(has_high)
        def _():
            fin_copy(i, 1, up).wait_send()

        mate_copy(i).wait_send()
        mate_block(i).wait_recv()
        return carry

    lax.fori_loop(0, count, drain, 0)
    w_copy.wait_send()
    g_copy.wait_send()
    for b in range(2):
        if nz > 1:
            for n in range(6):
                z_copy(b, n).wait_send()
        for d in range(nz):
            for e in range(1, nx):
                x_copy(b, d, e).wait_send()
            for f in range(1, ny):
                y_copy(b, d, f).wait_send()


def shards(cap, pre_act, w_out, b_out, row_slot, ctx_slot, text_rows, cotangent):
    nx, nz, ny, nl = (lax.axis_size(a) for a in ("x", "zh", "y", "zl"))
    xx, zh, yy = (lax.axis_index(a) for a in ("x", "zh", "y"))
    rows, depth = pre_act.shape
    tokens, width = cotangent.shape
    hidden = gelu_value(pre_act.astype(jnp.float32)).astype(jnp.bfloat16)
    merged = (
        jnp.dot(hidden, w_out, preferred_element_type=jnp.float32) + b_out.astype(jnp.float32)
    ).astype(jnp.bfloat16)

    def position(values, sign):
        peer, slot = values // cap, values % cap
        dx = (sign * (peer // (nz * ny) - xx)) % nx
        dz = (sign * ((peer // ny) % nz - zh)) % nz
        dy = (sign * (peer % ny - yy)) % ny
        base = ((dz * nx + dx) * ny + dy) * 2 * cap + slot
        return jnp.where(values >= 0, base, -1000000)

    row_out = position(row_slot, 1).reshape(1, rows)
    tok_out = position(ctx_slot, 1).reshape(1, tokens)
    row_in = position(row_slot, -1).reshape(rows, 1)
    tok_in = position(ctx_slot, -1).reshape(tokens, 1)

    half_width, half_rows = width // 2, rows // 2
    piece = depth // CHUNKS
    block = (nx, ny, 2 * cap, half_width)
    dma = pltpu.SemaphoreType.DMA
    bf16 = jnp.bfloat16
    scratch = [
        pltpu.VMEM((2, nz, *block), bf16),
        pltpu.VMEM((2, max(nz - 1, 1), *block), bf16),
        pltpu.VMEM((2, 2, max(nx // 2, 1), *block[1:]), bf16),
        pltpu.VMEM((2, nz, *block), bf16),
        pltpu.VMEM((2, nz, *block), bf16),
        pltpu.VMEM((depth, width), bf16),
        pltpu.VMEM((rows, width), bf16),
        pltpu.VMEM((half_rows, width), bf16),
        pltpu.VMEM((2, CHUNKS, half_rows, piece), bf16),
        pltpu.VMEM((CHUNKS, half_rows, piece), bf16),
        pltpu.VMEM((half_rows, piece), jnp.float32),
        dma((2, 6)), dma((2, 6)),
        dma((2, nz, nx)), dma((2, nz, nx)),
        dma((2, nz, ny)), dma((2, nz, ny)),
        dma, dma, dma, dma,
        dma((CHUNKS,)), dma((2, CHUNKS)),
        dma((2, CHUNKS)), dma((CHUNKS,)),
        dma((CHUNKS,)), dma((CHUNKS,)),
    ]
    return pl.pallas_call(
        functools.partial(kernel, (nz, nx, ny, nl), cap),
        out_shape=(
            jax.ShapeDtypeStruct((tokens, width), bf16),
            jax.ShapeDtypeStruct((rows, depth), bf16),
        ),
        in_specs=[pl.BlockSpec(memory_space=pltpu.VMEM)] * 9,
        out_specs=(pl.BlockSpec(memory_space=pltpu.VMEM),) * 2,
        scratch_shapes=scratch,
        compiler_params=pltpu.CompilerParams(
            collective_id=0, has_side_effects=True, vmem_limit_bytes=60 << 20
        ),
    )(merged, cotangent, text_rows, w_out, pre_act, row_out, tok_out, row_in, tok_in)


def build(mesh, nx, nz, nl, cap):
    split = Mesh(
        mesh.devices.reshape(nx, nz, nl, 2, mesh.shape["grp"]), ("x", "zh", "zl", "core", "y")
    )
    ctx, tp = ("x", "zh", "y"), ("zl", "core")
    return jax.shard_map(
        functools.partial(shards, cap),
        mesh=split,
        in_specs=(P(ctx, None), P(None, tp), P(tp), P(ctx), P(ctx), P(ctx, tp), P(ctx, tp)),
        out_specs=(P(ctx, tp), P(ctx, None)),
        check_vma=False,
    )


def solution(mesh):
    return build(mesh, 4, mesh.shape["ctx"] // 4, mesh.shape["tp"] // 2, 8)
```

```python
import functools

import jax
import jax.numpy as jnp
from jax import lax
from jax.experimental import pallas as pl
from jax.experimental.pallas import tpu as pltpu
from jax.sharding import Mesh
from jax.sharding import PartitionSpec as P

MESH = pl.DeviceIdType.MESH
CHUNKS = 40
LAG = 8


def gelu_value(values):
    return 0.5 * values * (1.0 + lax.erf(values * 0.7071067811865476))


def gelu_slope(values):
    return (
        0.5 * (1.0 + lax.erf(values * 0.7071067811865476))
        + values * jnp.exp(-0.5 * values * values) * 0.3989422804014327
    )


def remote(src, dst, send, recv, peer):
    return pltpu.make_async_remote_copy(
        src_ref=src, dst_ref=dst, send_sem=send, recv_sem=recv, device_id=peer, device_id_type=MESH
    )


def nt_dot(left, right):
    return lax.dot_general(
        left, right, (((1,), (1,)), ((), ())), preferred_element_type=jnp.float32
    )


def kernel(
    sizes, cap,
    cot_hbm, text_hbm, w_hbm, pre_hbm, bias, row_slot, tok_slot,
    emb_hbm, grad_hbm,
    cot, text, w, pre, merged, emb, grad, load_sem, store_sem,
    out_buf, z_buf, relay, x_buf, y_buf, w_far, rows_full, rows_far, flow_in, flow_out, acc,
    z_send, z_recv, part_send, part_recv, tail_send, tail_recv, x_send, x_recv, y_send, y_recv,
    w_send, w_recv, g_send, g_recv,
    flow_send, flow_recv, fin_send, fin_recv, mate_send, mate_recv,
):
    nz, nx, ny, nl = sizes
    zh, xx, yy = lax.axis_index("zh"), lax.axis_index("x"), lax.axis_index("y")
    line, core = lax.axis_index("zl"), lax.axis_index("core")
    mate = {"core": 1 - core}
    right, left = {"zh": lax.rem(zh + 1, nz)}, {"zh": lax.rem(zh + nz - 1, nz)}
    up, down = {"zl": line + 1}, {"zl": line - 1}
    x_peer = [{"x": lax.rem(xx + e, nx)} for e in range(nx)]
    y_peer = [{"y": lax.rem(yy + f, ny)} for f in range(ny)]
    blocks = nz * nx * ny
    slots = blocks * 2 * cap
    tokens, width = cot.shape
    half_width = width // 2
    rows, depth = pre.shape
    half_rows = rows // 2
    count, piece = flow_out.shape[0], flow_out.shape[2]
    shape6 = (nz, nx, ny, 2 * cap, half_width)

    middle = nl // 2 - 1 + core if nl > 1 else 0 * core
    has_low = jnp.logical_and(line <= middle, line > 0)
    has_high = jnp.logical_and(line >= middle, line < nl - 1)

    barrier = pltpu.get_barrier_semaphore()
    greeted = [mate] + x_peer[1:] + y_peer[1:]
    if nz > 1:
        greeted += [right, left]
    for peer in greeted:
        pl.semaphore_signal(barrier, inc=1, device_id=peer, device_id_type=MESH)

    @pl.when(line > 0)
    def _():
        pl.semaphore_signal(barrier, inc=1, device_id=down, device_id_type=MESH)

    @pl.when(line < nl - 1)
    def _():
        pl.semaphore_signal(barrier, inc=1, device_id=up, device_id_type=MESH)

    loads = [
        pltpu.make_async_copy(src, dst, load_sem.at[n])
        for n, (src, dst) in enumerate(
            ((cot_hbm, cot), (w_hbm, w), (pre_hbm, pre), (text_hbm, text))
        )
    ]
    for load in loads:
        load.start()

    def bits(n):
        return n.bit_length() - 1

    def position(values, sign):
        peer = lax.shift_right_logical(values, bits(cap))
        dy = (sign * ((peer & (ny - 1)) - yy)) & (ny - 1)
        dz = (sign * ((lax.shift_right_logical(peer, bits(ny)) & (nz - 1)) - zh)) & (nz - 1)
        dx = (sign * (lax.shift_right_logical(peer, bits(ny * nz)) - xx)) & (nx - 1)
        base = ((dz * nx + dx) * ny + dy) * (2 * cap) + (values & (cap - 1))
        return jnp.where(values >= 0, base, -1000000)

    def upright(values):
        wide = jnp.broadcast_to(values, (128, values.shape[1]))
        return jnp.transpose(wide)[:, :1]

    def place(b, source, where):
        total = jnp.zeros((slots, half_width), jnp.float32)
        ids = lax.broadcasted_iota(jnp.int32, (slots, source.shape[0]), 0)
        for h in range(2):
            hot = (ids == where + h * cap).astype(jnp.bfloat16)
            part = source[:, h * half_width : (h + 1) * half_width]
            total += jnp.dot(hot, part, preferred_element_type=jnp.float32)
        out_buf[b] = total.astype(jnp.bfloat16).reshape(shape6)

    def pick(b, where, h):
        ids = lax.broadcasted_iota(jnp.int32, (where.shape[0], slots), 1)
        hot = (ids == where + h * cap).astype(jnp.bfloat16)
        data = y_buf[b].reshape(slots, half_width)
        return jnp.dot(hot, data, preferred_element_type=jnp.float32)

    wait_peers = (
        len(greeted) + (line > 0).astype(jnp.int32) + (line < nl - 1).astype(jnp.int32)
    )
    cut = nx // 2
    parts, tails = nx * ny, cut * ny

    def z_copy(b, n):
        src, dst, peer = (
            lambda: (out_buf.at[b, 2, :cut], relay.at[b, 0], right),
            lambda: (out_buf.at[b, 2, cut:], relay.at[b, 1], left),
            lambda: (out_buf.at[b, 1], z_buf.at[b, 0], right),
            lambda: (out_buf.at[b, 3], z_buf.at[b, 2], left),
            lambda: (relay.at[b, 0], z_buf.at[b, 1, :cut], right),
            lambda: (relay.at[b, 1], z_buf.at[b, 1, cut:], left),
        )[n]()
        return remote(src, dst, z_send.at[b, n], z_recv.at[b, n], peer)

    def x_copy(b, d, e):
        src = out_buf.at[b, 0, e] if d == 0 else z_buf.at[b, d - 1, e]
        dst = x_buf.at[b, d, e]
        if e == 0:
            return pltpu.make_async_copy(src, dst, x_recv.at[b, d, 0])
        return remote(src, dst, x_send.at[b, d, e], x_recv.at[b, d, e], x_peer[e])

    def y_copy(b, d, f):
        src, dst = x_buf.at[b, d, :, f], y_buf.at[b, d, :, f]
        if f == 0:
            return pltpu.make_async_copy(src, dst, y_recv.at[b, d, 0])
        return remote(src, dst, y_send.at[b, d, f], y_recv.at[b, d, f], y_peer[f])

    def part_copy(q, side):
        e, f = q // ny, q % ny
        src, dst = (out_buf.at[1, 1 + 2 * side, e, f], z_buf.at[1, 2 * side, e, f])
        return remote(
            src, dst, part_send.at[side, q], part_recv.at[side, q], (right, left)[side]
        )

    def tail_copy(q, side):
        e, f = q // ny, q % ny
        src, dst = relay.at[1, side, e, f], z_buf.at[1, 1, side * cut + e, f]
        return remote(
            src, dst, tail_send.at[side, q], tail_recv.at[side, q], (right, left)[side]
        )

    def each(count, act):
        def body(q, carry):
            for side in range(2):
                act(q, side)
            return carry

        lax.fori_loop(0, count, body, 0)

    def z_start(names):
        if nz > 1:
            for b, n in names:
                z_copy(b, n).start()

    def z_forward():
        if nz > 1:
            for n in (0, 1):
                z_copy(0, n).wait_recv()
                z_copy(0, n + 4).start()

    def z_arrive(d):
        for n in {1: (2,), 2: (4, 5), 3: (3,)}[d]:
            z_copy(0, n).wait_recv()

    def x_start(b, d):
        for e in list(range(1, nx)) + [0]:
            x_copy(b, d, e).start()

    def y_start(b, d):
        x_copy(b, d, 0).wait()
        for e in range(1, nx):
            x_copy(b, d, e).wait_recv()
        for f in list(range(1, ny)) + [0]:
            y_copy(b, d, f).start()

    def y_arrive(b, d):
        y_copy(b, d, 0).wait()
        for f in range(1, ny):
            y_copy(b, d, f).wait_recv()

    w_copy = remote(w, w_far, w_send, w_recv, mate)
    tok_out = position(tok_slot[...], 1)
    loads[0].wait()
    place(0, cot, tok_out)
    pl.semaphore_wait(barrier, wait_peers)
    z_start([(0, n) for n in range(4)])
    x_start(0, 0)
    loads[1].wait()
    w_copy.start()
    loads[2].wait()
    merged[...] = jnp.zeros_like(merged)
    deep = 4 * piece

    def forward(i, carry):
        cols = pl.ds(pl.multiple_of(i * deep, deep), deep)
        hidden = gelu_value(pre[:, cols].astype(jnp.float32)).astype(jnp.bfloat16)
        merged[...] += jnp.dot(hidden, w[cols, :], preferred_element_type=jnp.float32)
        return carry

    lax.fori_loop(0, depth // deep, forward, 0)
    place(
        1,
        (merged[...] + bias[...].astype(jnp.float32)).astype(jnp.bfloat16),
        position(row_slot[...], 1),
    )
    y_start(0, 0)
    z_forward()
    z_start([(1, 0), (1, 1)])
    x_start(1, 0)
    row_in = upright(position(row_slot[...], -1))
    tok_in = upright(position(tok_slot[...], -1))
    y_start(1, 0)
    if nz > 1:
        for d in (1, 3):
            z_arrive(d)
            x_start(0, d)
        for d in (1, 3):
            y_start(0, d)
        z_arrive(2)
        x_start(0, 2)
        y_start(0, 2)
    for d in range(nz):
        y_arrive(0, d)

    for h in range(2):
        rows_full[:, h * half_width : (h + 1) * half_width] = pick(0, row_in, h).astype(
            jnp.bfloat16
        )
    mine = pl.ds(pl.multiple_of(core * half_rows, half_rows), half_rows)
    other = pl.ds(pl.multiple_of((1 - core) * half_rows, half_rows), half_rows)
    g_copy = remote(rows_full.at[other], rows_far, g_send, g_recv, mate)
    g_copy.start()
    w_copy.wait_recv()
    g_copy.wait_recv()

    def columns(i):
        return pl.ds(pl.multiple_of(i * piece, piece), piece)

    def flow_copy(i, side, peer):
        return remote(
            flow_out.at[i], flow_in.at[side, i], flow_send.at[i], flow_recv.at[side, i], peer
        )

    def fin_copy(i, side, peer):
        block = grad.at[mine, columns(i)]
        return remote(block, block, fin_send.at[side, i], fin_recv.at[i], peer)

    def mate_copy(i):
        block = grad.at[mine, columns(i)]
        return remote(block, block, mate_send.at[i], mate_recv.at[i], mate)

    def mate_block(i):
        block = grad.at[other, columns(i)]
        return remote(block, block, mate_send.at[i], mate_recv.at[i], mate)

    def publish(i):
        @pl.when(has_low)
        def _():
            fin_copy(i, 0, down).start()

        @pl.when(has_high)
        def _():
            fin_copy(i, 1, up).start()

        mate_copy(i).start()

    away = jnp.where(line < middle, middle - line, line - middle)
    lag = 1 + LAG * away
    steps = count + 1 + LAG * (nl // 2 + (1 if nl > 1 else 0))

    def dispatch(i):
        @pl.when(i < parts)
        def _():
            for side in range(2):
                part_copy(i, side).start()

        @pl.when(i == parts)
        def _():
            for n in (0, 1):
                z_copy(1, n).wait_recv()

        @pl.when(jnp.logical_and(i >= parts, i < parts + tails))
        def _():
            for side in range(2):
                tail_copy(i - parts, side).start()

    def step(i, carry):
        if nz > 1:
            dispatch(i)

        @pl.when(i < count)
        def _():
            acc[...] = nt_dot(rows_full[mine, :], w[columns(i), :]) + nt_dot(
                rows_far[...], w_far[columns(i), :]
            )

            @pl.when(has_low)
            def _():
                flow_copy(i, 0, up).wait_recv()
                acc[...] += flow_in[0, i].astype(jnp.float32)

            @pl.when(has_high)
            def _():
                flow_copy(i, 1, down).wait_recv()
                acc[...] += flow_in[1, i].astype(jnp.float32)

            @pl.when(line != middle)
            def _():
                flow_out[i] = acc[...].astype(jnp.bfloat16)

            @pl.when(line < middle)
            def _():
                flow_copy(i, 0, up).start()

            @pl.when(line > middle)
            def _():
                flow_copy(i, 1, down).start()

            @pl.when(line == middle)
            def _():
                slope = gelu_slope(pre[mine, columns(i)].astype(jnp.float32))
                grad[mine, columns(i)] = (acc[...] * slope).astype(jnp.bfloat16)
                publish(i)

        j = i - lag

        @pl.when(jnp.logical_and(line != middle, jnp.logical_and(j >= 0, j < count)))
        def _():
            fin_copy(j, 0, down).wait_recv()
            publish(j)

        return carry

    first = parts + tails + 6
    marks = (0, first, first + 5, first + 9, steps)
    lax.fori_loop(marks[0], marks[1], step, 0)
    if nz > 1:
        each(parts, lambda q, side: part_copy(q, side).wait_recv())
        for d in (1, 3):
            x_start(1, d)
    lax.fori_loop(marks[1], marks[2], step, 0)
    if nz > 1:
        for d in (1, 3):
            y_start(1, d)
        each(tails, lambda q, side: tail_copy(q, side).wait_recv())
        x_start(1, 2)
    lax.fori_loop(marks[2], marks[3], step, 0)
    if nz > 1:
        y_start(1, 2)
    lax.fori_loop(marks[3], steps, step, 0)

    loads[3].wait()
    for d in range(nz):
        y_arrive(1, d)
    for h in range(2):
        part = pl.ds(h * half_width, half_width)
        emb[:, part] = jnp.where(
            tok_in >= 0, pick(1, tok_in, h).astype(jnp.bfloat16), text[:, part]
        )

    emb_store = pltpu.make_async_copy(emb, emb_hbm, store_sem.at[0])
    emb_store.start()

    def drain(i, carry):
        @pl.when(line < middle)
        def _():
            flow_copy(i, 0, up).wait_send()

        @pl.when(line > middle)
        def _():
            flow_copy(i, 1, down).wait_send()

        @pl.when(has_low)
        def _():
            fin_copy(i, 0, down).wait_send()

        @pl.when(has_high)
        def _():
            fin_copy(i, 1, up).wait_send()

        mate_copy(i).wait_send()
        mate_block(i).wait_recv()
        return carry

    groups = 4
    span = count // groups
    stores = []
    for n in range(groups):
        lax.fori_loop(n * span, (n + 1) * span, drain, 0)
        cols = pl.ds(n * span * piece, span * piece)
        store = pltpu.make_async_copy(grad.at[:, cols], grad_hbm.at[:, cols], store_sem.at[n + 1])
        store.start()
        stores.append(store)
    w_copy.wait_send()
    g_copy.wait_send()
    if nz > 1:
        for n in range(6):
            z_copy(0, n).wait_send()
        for n in range(2):
            z_copy(1, n).wait_send()
        each(parts, lambda q, side: part_copy(q, side).wait_send())
        each(tails, lambda q, side: tail_copy(q, side).wait_send())
    for b in range(2):
        for d in range(nz):
            for e in range(1, nx):
                x_copy(b, d, e).wait_send()
            for f in range(1, ny):
                y_copy(b, d, f).wait_send()
    emb_store.wait()
    for store in stores:
        store.wait()


def shards(cap, pre_act, w_out, b_out, row_slot, ctx_slot, text_rows, cotangent):
    nx, nz, ny, nl = (lax.axis_size(a) for a in ("x", "zh", "y", "zl"))
    rows, depth = pre_act.shape
    tokens, width = cotangent.shape
    half_width, half_rows = width // 2, rows // 2
    piece = depth // CHUNKS
    block = (nx, ny, 2 * cap, half_width)
    dma = pltpu.SemaphoreType.DMA
    bf16 = jnp.bfloat16
    scratch = [
        pltpu.VMEM((tokens, width), bf16),
        pltpu.VMEM((tokens, width), bf16),
        pltpu.VMEM((depth, width), bf16),
        pltpu.VMEM((rows, depth), bf16),
        pltpu.VMEM((rows, width), jnp.float32),
        pltpu.VMEM((tokens, width), bf16),
        pltpu.VMEM((rows, depth), bf16),
        dma((4,)), dma((5,)),
        pltpu.VMEM((2, nz, *block), bf16),
        pltpu.VMEM((2, max(nz - 1, 1), *block), bf16),
        pltpu.VMEM((2, 2, max(nx // 2, 1), *block[1:]), bf16),
        pltpu.VMEM((2, nz, *block), bf16),
        pltpu.VMEM((2, nz, *block), bf16),
        pltpu.VMEM((depth, width), bf16),
        pltpu.VMEM((rows, width), bf16),
        pltpu.VMEM((half_rows, width), bf16),
        pltpu.VMEM((2, CHUNKS, half_rows, piece), bf16),
        pltpu.VMEM((CHUNKS, half_rows, piece), bf16),
        pltpu.VMEM((half_rows, piece), jnp.float32),
        dma((2, 6)), dma((2, 6)),
        dma((2, nx * ny)), dma((2, nx * ny)),
        dma((2, max(nx // 2 * ny, 1))), dma((2, max(nx // 2 * ny, 1))),
        dma((2, nz, nx)), dma((2, nz, nx)),
        dma((2, nz, ny)), dma((2, nz, ny)),
        dma, dma, dma, dma,
        dma((CHUNKS,)), dma((2, CHUNKS)),
        dma((2, CHUNKS)), dma((CHUNKS,)),
        dma((CHUNKS,)), dma((CHUNKS,)),
    ]
    return pl.pallas_call(
        functools.partial(kernel, (nz, nx, ny, nl), cap),
        out_shape=(
            jax.ShapeDtypeStruct((tokens, width), bf16),
            jax.ShapeDtypeStruct((rows, depth), bf16),
        ),
        in_specs=[pl.BlockSpec(memory_space=pl.ANY)] * 4
        + [pl.BlockSpec(memory_space=pltpu.VMEM)] * 3,
        out_specs=(pl.BlockSpec(memory_space=pl.ANY),) * 2,
        scratch_shapes=scratch,
        compiler_params=pltpu.CompilerParams(
            collective_id=0, has_side_effects=True, vmem_limit_bytes=60 << 20
        ),
    )(
        cotangent, text_rows, w_out, pre_act,
        b_out.reshape(1, width), row_slot.reshape(1, rows), ctx_slot.reshape(1, tokens),
    )


def build(mesh, nx, nz, nl, cap):
    split = Mesh(
        mesh.devices.reshape(nx, nz, nl, 2, mesh.shape["grp"]), ("x", "zh", "zl", "core", "y")
    )
    ctx, tp = ("x", "zh", "y"), ("zl", "core")
    return jax.shard_map(
        functools.partial(shards, cap),
        mesh=split,
        in_specs=(P(ctx, None), P(None, tp), P(tp), P(ctx), P(ctx), P(ctx, tp), P(ctx, tp)),
        out_specs=(P(ctx, tp), P(ctx, None)),
        check_vma=False,
    )


def solution(mesh):
    return build(mesh, 4, mesh.shape["ctx"] // 4, mesh.shape["tp"] // 2, 8)
```

```python
import functools

import jax
import jax.numpy as jnp
from jax import lax
from jax.experimental import pallas as pl
from jax.experimental.pallas import tpu as pltpu
from jax.sharding import Mesh
from jax.sharding import PartitionSpec as P

MESH = pl.DeviceIdType.MESH
CHUNKS = 40
LAG = 8
EARLY = 10


def gelu_value(values):
    return 0.5 * values * (1.0 + lax.erf(values * 0.7071067811865476))


def gelu_slope(values):
    return (
        0.5 * (1.0 + lax.erf(values * 0.7071067811865476))
        + values * jnp.exp(-0.5 * values * values) * 0.3989422804014327
    )


def remote(src, dst, send, recv, peer):
    return pltpu.make_async_remote_copy(
        src_ref=src, dst_ref=dst, send_sem=send, recv_sem=recv, device_id=peer, device_id_type=MESH
    )


def nt_dot(left, right):
    return lax.dot_general(
        left, right, (((1,), (1,)), ((), ())), preferred_element_type=jnp.float32
    )


def kernel(
    sizes, cap,
    cot_hbm, text_hbm, w_hbm, pre_hbm, bias, row_slot, tok_slot,
    emb_hbm, grad_hbm,
    cot, text, w, pre, merged, emb, grad, load_sem, store_sem,
    out_buf, z_buf, relay, x_buf, y_buf, w_far, rows_full, rows_far, flow_in, flow_out, acc,
    z_send, z_recv, x_send, x_recv, y_send, y_recv,
    w_send, w_recv, g_send, g_recv,
    flow_send, flow_recv, fin_send, fin_recv, mate_send, mate_recv,
):
    nz, nx, ny, nl = sizes
    zh, xx, yy = lax.axis_index("zh"), lax.axis_index("x"), lax.axis_index("y")
    line, core = lax.axis_index("zl"), lax.axis_index("core")
    mate = {"core": 1 - core}
    right, left = {"zh": lax.rem(zh + 1, nz)}, {"zh": lax.rem(zh + nz - 1, nz)}
    up, down = {"zl": line + 1}, {"zl": line - 1}
    x_peer = [{"x": lax.rem(xx + e, nx)} for e in range(nx)]
    y_peer = [{"y": lax.rem(yy + f, ny)} for f in range(ny)]
    blocks = nz * nx * ny
    slots = blocks * 2 * cap
    tokens, width = cot.shape
    half_width = width // 2
    rows, depth = pre.shape
    half_rows = rows // 2
    count, piece = flow_out.shape[0], flow_out.shape[2]
    shape6 = (nz, nx, ny, 2 * cap, half_width)

    middle = nl // 2 - 1 + core if nl > 1 else 0 * core
    has_low = jnp.logical_and(line <= middle, line > 0)
    has_high = jnp.logical_and(line >= middle, line < nl - 1)

    barrier = pltpu.get_barrier_semaphore()
    greeted = [mate] + x_peer[1:] + y_peer[1:]
    if nz > 1:
        greeted += [right, left]
    for peer in greeted:
        pl.semaphore_signal(barrier, inc=1, device_id=peer, device_id_type=MESH)

    @pl.when(line > 0)
    def _():
        pl.semaphore_signal(barrier, inc=1, device_id=down, device_id_type=MESH)

    @pl.when(line < nl - 1)
    def _():
        pl.semaphore_signal(barrier, inc=1, device_id=up, device_id_type=MESH)

    loads = [
        pltpu.make_async_copy(src, dst, load_sem.at[n])
        for n, (src, dst) in enumerate(
            ((cot_hbm, cot), (w_hbm, w), (pre_hbm, pre), (text_hbm, text))
        )
    ]
    for load in loads:
        load.start()

    def bits(n):
        return n.bit_length() - 1

    def position(values, sign):
        peer = lax.shift_right_logical(values, bits(cap))
        dy = (sign * ((peer & (ny - 1)) - yy)) & (ny - 1)
        dz = (sign * ((lax.shift_right_logical(peer, bits(ny)) & (nz - 1)) - zh)) & (nz - 1)
        dx = (sign * (lax.shift_right_logical(peer, bits(ny * nz)) - xx)) & (nx - 1)
        base = ((dz * nx + dx) * ny + dy) * (2 * cap) + (values & (cap - 1))
        return jnp.where(values >= 0, base, -1000000)

    def upright(values):
        wide = jnp.broadcast_to(values, (128, values.shape[1]))
        return jnp.transpose(wide)[:, :1]

    def place(b, source, where):
        total = jnp.zeros((slots, half_width), jnp.float32)
        ids = lax.broadcasted_iota(jnp.int32, (slots, source.shape[0]), 0)
        for h in range(2):
            hot = (ids == where + h * cap).astype(jnp.bfloat16)
            part = source[:, h * half_width : (h + 1) * half_width]
            total += jnp.dot(hot, part, preferred_element_type=jnp.float32)
        out_buf[b] = total.astype(jnp.bfloat16).reshape(shape6)

    def pick(b, where, h):
        ids = lax.broadcasted_iota(jnp.int32, (where.shape[0], slots), 1)
        hot = (ids == where + h * cap).astype(jnp.bfloat16)
        data = y_buf[b].reshape(slots, half_width)
        return jnp.dot(hot, data, preferred_element_type=jnp.float32)

    wait_peers = (
        len(greeted) + (line > 0).astype(jnp.int32) + (line < nl - 1).astype(jnp.int32)
    )
    cut = nx // 2

    def z_copy(b, n):
        src, dst, peer = (
            lambda: (out_buf.at[b, 2, :cut], relay.at[b, 0], right),
            lambda: (out_buf.at[b, 2, cut:], relay.at[b, 1], left),
            lambda: (out_buf.at[b, 1], z_buf.at[b, 0], right),
            lambda: (out_buf.at[b, 3], z_buf.at[b, 2], left),
            lambda: (relay.at[b, 0], z_buf.at[b, 1, :cut], right),
            lambda: (relay.at[b, 1], z_buf.at[b, 1, cut:], left),
        )[n]()
        return remote(src, dst, z_send.at[b, n], z_recv.at[b, n], peer)

    def x_copy(b, d, e):
        src = out_buf.at[b, 0, e] if d == 0 else z_buf.at[b, d - 1, e]
        dst = x_buf.at[b, d, e]
        if e == 0:
            return pltpu.make_async_copy(src, dst, x_recv.at[b, d, 0])
        return remote(src, dst, x_send.at[b, d, e], x_recv.at[b, d, e], x_peer[e])

    def y_copy(b, d, f):
        src, dst = x_buf.at[b, d, :, f], y_buf.at[b, d, :, f]
        if f == 0:
            return pltpu.make_async_copy(src, dst, y_recv.at[b, d, 0])
        return remote(src, dst, y_send.at[b, d, f], y_recv.at[b, d, f], y_peer[f])

    def z_start(names):
        if nz > 1:
            for b, n in names:
                z_copy(b, n).start()

    def z_forward():
        if nz > 1:
            for n in (0, 1):
                z_copy(0, n).wait_recv()
                z_copy(0, n + 4).start()

    def z_arrive(b, d):
        for n in {1: (2,), 2: (4, 5), 3: (3,)}[d]:
            z_copy(b, n).wait_recv()

    def x_start(b, d):
        for e in list(range(1, nx)) + [0]:
            x_copy(b, d, e).start()

    def y_start(b, d):
        x_copy(b, d, 0).wait()
        for e in range(1, nx):
            x_copy(b, d, e).wait_recv()
        for f in list(range(1, ny)) + [0]:
            y_copy(b, d, f).start()

    def y_arrive(b, d):
        y_copy(b, d, 0).wait()
        for f in range(1, ny):
            y_copy(b, d, f).wait_recv()

    w_copy = remote(w, w_far, w_send, w_recv, mate)
    tok_out = position(tok_slot[...], 1)
    loads[0].wait()
    place(0, cot, tok_out)
    pl.semaphore_wait(barrier, wait_peers)
    z_start([(0, n) for n in range(4)])
    x_start(0, 0)
    loads[1].wait()
    w_copy.start()
    loads[2].wait()
    merged[...] = jnp.zeros_like(merged)
    deep = 4 * piece

    def forward(i, carry):
        cols = pl.ds(pl.multiple_of(i * deep, deep), deep)
        hidden = gelu_value(pre[:, cols].astype(jnp.float32)).astype(jnp.bfloat16)
        merged[...] += jnp.dot(hidden, w[cols, :], preferred_element_type=jnp.float32)
        return carry

    lax.fori_loop(0, depth // deep, forward, 0)
    place(
        1,
        (merged[...] + bias[...].astype(jnp.float32)).astype(jnp.bfloat16),
        position(row_slot[...], 1),
    )
    y_start(0, 0)
    z_forward()
    z_start([(1, 0), (1, 1)])
    low = line <= middle
    high = line > middle

    def outward(right_copy, left_copy, relays):
        def go(n, relayed):
            if relays:
                z_copy(1, relayed).wait_recv()
            z_copy(1, n).start()

        @pl.when(low)
        def _():
            go(left_copy, 1)

        @pl.when(high)
        def _():
            go(right_copy, 0)

    def inward(right_copy, left_copy, relays):
        def go(n, relayed):
            if relays:
                z_copy(1, relayed).wait_recv()
            z_copy(1, n).start()

        @pl.when(low)
        def _():
            go(right_copy, 0)

        @pl.when(high)
        def _():
            go(left_copy, 1)

    if nz > 1:
        outward(2, 3, False)
    x_start(1, 0)
    row_in = upright(position(row_slot[...], -1))
    tok_in = upright(position(tok_slot[...], -1))
    y_start(1, 0)
    if nz > 1:
        for d in (1, 3):
            z_arrive(0, d)
            x_start(0, d)
        for d in (1, 3):
            y_start(0, d)
        z_arrive(0, 2)
        x_start(0, 2)
        y_start(0, 2)
    for d in range(nz):
        y_arrive(0, d)

    for h in range(2):
        rows_full[:, h * half_width : (h + 1) * half_width] = pick(0, row_in, h).astype(
            jnp.bfloat16
        )
    mine = pl.ds(pl.multiple_of(core * half_rows, half_rows), half_rows)
    other = pl.ds(pl.multiple_of((1 - core) * half_rows, half_rows), half_rows)
    g_copy = remote(rows_full.at[other], rows_far, g_send, g_recv, mate)
    g_copy.start()
    w_copy.wait_recv()
    g_copy.wait_recv()

    def columns(i):
        return pl.ds(pl.multiple_of(i * piece, piece), piece)

    def flow_copy(i, side, peer):
        return remote(
            flow_out.at[i], flow_in.at[side, i], flow_send.at[i], flow_recv.at[side, i], peer
        )

    def fin_copy(i, side, peer):
        block = grad.at[mine, columns(i)]
        return remote(block, block, fin_send.at[side, i], fin_recv.at[i], peer)

    def mate_copy(i):
        block = grad.at[mine, columns(i)]
        return remote(block, block, mate_send.at[i], mate_recv.at[i], mate)

    def mate_block(i):
        block = grad.at[other, columns(i)]
        return remote(block, block, mate_send.at[i], mate_recv.at[i], mate)

    def publish(i):
        @pl.when(has_low)
        def _():
            fin_copy(i, 0, down).start()

        @pl.when(has_high)
        def _():
            fin_copy(i, 1, up).start()

        mate_copy(i).start()

    away = jnp.where(line < middle, middle - line, line - middle)
    lag = 1 + LAG * away
    steps = count + 1 + LAG * (nl // 2 + (1 if nl > 1 else 0))

    def dispatch(i):
        @pl.when(i == EARLY)
        def _():
            outward(4, 5, True)

        @pl.when(i == count)
        def _():
            inward(2, 3, False)
            inward(4, 5, True)

    def step(i, carry):
        if nz > 1:
            dispatch(i)

        @pl.when(i < count)
        def _():
            acc[...] = nt_dot(rows_full[mine, :], w[columns(i), :]) + nt_dot(
                rows_far[...], w_far[columns(i), :]
            )

            @pl.when(has_low)
            def _():
                flow_copy(i, 0, up).wait_recv()
                acc[...] += flow_in[0, i].astype(jnp.float32)

            @pl.when(has_high)
            def _():
                flow_copy(i, 1, down).wait_recv()
                acc[...] += flow_in[1, i].astype(jnp.float32)

            @pl.when(line != middle)
            def _():
                flow_out[i] = acc[...].astype(jnp.bfloat16)

            @pl.when(line < middle)
            def _():
                flow_copy(i, 0, up).start()

            @pl.when(line > middle)
            def _():
                flow_copy(i, 1, down).start()

            @pl.when(line == middle)
            def _():
                slope = gelu_slope(pre[mine, columns(i)].astype(jnp.float32))
                grad[mine, columns(i)] = (acc[...] * slope).astype(jnp.bfloat16)
                publish(i)

        j = i - lag

        @pl.when(jnp.logical_and(line != middle, jnp.logical_and(j >= 0, j < count)))
        def _():
            fin_copy(j, 0, down).wait_recv()
            publish(j)

        return carry

    lax.fori_loop(0, steps, step, 0)
    if nz > 1:
        for d in (1, 3):
            z_arrive(1, d)
            x_start(1, d)
        for d in (1, 3):
            y_start(1, d)
        z_arrive(1, 2)
        x_start(1, 2)
        y_start(1, 2)

    loads[3].wait()
    for d in range(nz):
        y_arrive(1, d)
    for h in range(2):
        part = pl.ds(h * half_width, half_width)
        emb[:, part] = jnp.where(
            tok_in >= 0, pick(1, tok_in, h).astype(jnp.bfloat16), text[:, part]
        )

    emb_store = pltpu.make_async_copy(emb, emb_hbm, store_sem.at[0])
    emb_store.start()

    def drain(i, carry):
        @pl.when(line < middle)
        def _():
            flow_copy(i, 0, up).wait_send()

        @pl.when(line > middle)
        def _():
            flow_copy(i, 1, down).wait_send()

        @pl.when(has_low)
        def _():
            fin_copy(i, 0, down).wait_send()

        @pl.when(has_high)
        def _():
            fin_copy(i, 1, up).wait_send()

        mate_copy(i).wait_send()
        mate_block(i).wait_recv()
        return carry

    groups = 4
    span = count // groups
    stores = []
    for n in range(groups):
        lax.fori_loop(n * span, (n + 1) * span, drain, 0)
        cols = pl.ds(n * span * piece, span * piece)
        store = pltpu.make_async_copy(grad.at[:, cols], grad_hbm.at[:, cols], store_sem.at[n + 1])
        store.start()
        stores.append(store)
    w_copy.wait_send()
    g_copy.wait_send()
    if nz > 1:
        for b in range(2):
            for n in range(6):
                z_copy(b, n).wait_send()
    for b in range(2):
        for d in range(nz):
            for e in range(1, nx):
                x_copy(b, d, e).wait_send()
            for f in range(1, ny):
                y_copy(b, d, f).wait_send()
    emb_store.wait()
    for store in stores:
        store.wait()


def shards(cap, pre_act, w_out, b_out, row_slot, ctx_slot, text_rows, cotangent):
    nx, nz, ny, nl = (lax.axis_size(a) for a in ("x", "zh", "y", "zl"))
    rows, depth = pre_act.shape
    tokens, width = cotangent.shape
    half_width, half_rows = width // 2, rows // 2
    piece = depth // CHUNKS
    block = (nx, ny, 2 * cap, half_width)
    dma = pltpu.SemaphoreType.DMA
    bf16 = jnp.bfloat16
    scratch = [
        pltpu.VMEM((tokens, width), bf16),
        pltpu.VMEM((tokens, width), bf16),
        pltpu.VMEM((depth, width), bf16),
        pltpu.VMEM((rows, depth), bf16),
        pltpu.VMEM((rows, width), jnp.float32),
        pltpu.VMEM((tokens, width), bf16),
        pltpu.VMEM((rows, depth), bf16),
        dma((4,)), dma((5,)),
        pltpu.VMEM((2, nz, *block), bf16),
        pltpu.VMEM((2, max(nz - 1, 1), *block), bf16),
        pltpu.VMEM((2, 2, max(nx // 2, 1), *block[1:]), bf16),
        pltpu.VMEM((2, nz, *block), bf16),
        pltpu.VMEM((2, nz, *block), bf16),
        pltpu.VMEM((depth, width), bf16),
        pltpu.VMEM((rows, width), bf16),
        pltpu.VMEM((half_rows, width), bf16),
        pltpu.VMEM((2, CHUNKS, half_rows, piece), bf16),
        pltpu.VMEM((CHUNKS, half_rows, piece), bf16),
        pltpu.VMEM((half_rows, piece), jnp.float32),
        dma((2, 6)), dma((2, 6)),
        dma((2, nz, nx)), dma((2, nz, nx)),
        dma((2, nz, ny)), dma((2, nz, ny)),
        dma, dma, dma, dma,
        dma((CHUNKS,)), dma((2, CHUNKS)),
        dma((2, CHUNKS)), dma((CHUNKS,)),
        dma((CHUNKS,)), dma((CHUNKS,)),
    ]
    return pl.pallas_call(
        functools.partial(kernel, (nz, nx, ny, nl), cap),
        out_shape=(
            jax.ShapeDtypeStruct((tokens, width), bf16),
            jax.ShapeDtypeStruct((rows, depth), bf16),
        ),
        in_specs=[pl.BlockSpec(memory_space=pl.ANY)] * 4
        + [pl.BlockSpec(memory_space=pltpu.VMEM)] * 3,
        out_specs=(pl.BlockSpec(memory_space=pl.ANY),) * 2,
        scratch_shapes=scratch,
        compiler_params=pltpu.CompilerParams(
            collective_id=0, has_side_effects=True, vmem_limit_bytes=60 << 20
        ),
    )(
        cotangent, text_rows, w_out, pre_act,
        b_out.reshape(1, width), row_slot.reshape(1, rows), ctx_slot.reshape(1, tokens),
    )


def build(mesh, nx, nz, nl, cap):
    split = Mesh(
        mesh.devices.reshape(nx, nz, nl, 2, mesh.shape["grp"]), ("x", "zh", "zl", "core", "y")
    )
    ctx, tp = ("x", "zh", "y"), ("zl", "core")
    return jax.shard_map(
        functools.partial(shards, cap),
        mesh=split,
        in_specs=(P(ctx, None), P(None, tp), P(tp), P(ctx), P(ctx), P(ctx, tp), P(ctx, tp)),
        out_specs=(P(ctx, tp), P(ctx, None)),
        check_vma=False,
    )


def solution(mesh):
    return build(mesh, 4, mesh.shape["ctx"] // 4, mesh.shape["tp"] // 2, 8)
```

```python
import functools

import jax
import jax.numpy as jnp
from jax import lax
from jax.experimental import pallas as pl
from jax.experimental.pallas import tpu as pltpu
from jax.sharding import Mesh
from jax.sharding import PartitionSpec as P

MESH = pl.DeviceIdType.MESH
CHUNKS = 40
LAG = 8


def gelu_value(values):
    return 0.5 * values * (1.0 + lax.erf(values * 0.7071067811865476))


def gelu_slope(values):
    return (
        0.5 * (1.0 + lax.erf(values * 0.7071067811865476))
        + values * jnp.exp(-0.5 * values * values) * 0.3989422804014327
    )


def remote(src, dst, send, recv, peer):
    return pltpu.make_async_remote_copy(
        src_ref=src, dst_ref=dst, send_sem=send, recv_sem=recv, device_id=peer, device_id_type=MESH
    )


def nt_dot(left, right):
    return lax.dot_general(
        left, right, (((1,), (1,)), ((), ())), preferred_element_type=jnp.float32
    )


def kernel(
    sizes, cap,
    cot_hbm, text_hbm, w_hbm, pre_hbm, bias, row_slot, tok_slot,
    emb_hbm, grad_hbm,
    cot, text, w, pre, merged, emb, grad, load_sem, store_sem,
    out_buf, z_buf, relay, x_buf, y_buf, w_far, rows_full, rows_far, flow_in, flow_out, acc,
    z_send, z_recv, x_send, x_recv, y_send, y_recv,
    w_send, w_recv, g_send, g_recv,
    flow_send, flow_recv, fin_send, fin_recv, mate_send, mate_recv,
):
    nz, nx, ny, nl = sizes
    zh, xx, yy = lax.axis_index("zh"), lax.axis_index("x"), lax.axis_index("y")
    line, core = lax.axis_index("zl"), lax.axis_index("core")
    mate = {"core": 1 - core}
    right, left = {"zh": lax.rem(zh + 1, nz)}, {"zh": lax.rem(zh + nz - 1, nz)}
    up, down = {"zl": line + 1}, {"zl": line - 1}
    x_peer = [{"x": lax.rem(xx + e, nx)} for e in range(nx)]
    y_peer = [{"y": lax.rem(yy + f, ny)} for f in range(ny)]
    blocks = nz * nx * ny
    slots = blocks * 2 * cap
    tokens, width = cot.shape
    half_width = width // 2
    rows, depth = pre.shape
    half_rows = rows // 2
    count, piece = flow_out.shape[0], flow_out.shape[2]
    shape6 = (nz, nx, ny, 2 * cap, half_width)

    middle = nl // 2 - 1 + core if nl > 1 else 0 * core
    has_low = jnp.logical_and(line <= middle, line > 0)
    has_high = jnp.logical_and(line >= middle, line < nl - 1)

    barrier = pltpu.get_barrier_semaphore()
    greeted = [mate] + x_peer[1:] + y_peer[1:]
    if nz > 1:
        greeted += [right, left]
    for peer in greeted:
        pl.semaphore_signal(barrier, inc=1, device_id=peer, device_id_type=MESH)

    @pl.when(line > 0)
    def _():
        pl.semaphore_signal(barrier, inc=1, device_id=down, device_id_type=MESH)

    @pl.when(line < nl - 1)
    def _():
        pl.semaphore_signal(barrier, inc=1, device_id=up, device_id_type=MESH)

    loads = [
        pltpu.make_async_copy(src, dst, load_sem.at[n])
        for n, (src, dst) in enumerate(
            ((cot_hbm, cot), (w_hbm, w), (pre_hbm, pre), (text_hbm, text))
        )
    ]
    for load in loads:
        load.start()

    def bits(n):
        return n.bit_length() - 1

    def position(values, sign):
        peer = lax.shift_right_logical(values, bits(cap))
        dy = (sign * ((peer & (ny - 1)) - yy)) & (ny - 1)
        dz = (sign * ((lax.shift_right_logical(peer, bits(ny)) & (nz - 1)) - zh)) & (nz - 1)
        dx = (sign * (lax.shift_right_logical(peer, bits(ny * nz)) - xx)) & (nx - 1)
        base = ((dz * nx + dx) * ny + dy) * (2 * cap) + (values & (cap - 1))
        return jnp.where(values >= 0, base, -1000000)

    def upright(values):
        wide = jnp.broadcast_to(values, (128, values.shape[1]))
        return jnp.transpose(wide)[:, :1]

    def place(b, source, where):
        total = jnp.zeros((slots, half_width), jnp.float32)
        ids = lax.broadcasted_iota(jnp.int32, (slots, source.shape[0]), 0)
        for h in range(2):
            hot = (ids == where + h * cap).astype(jnp.bfloat16)
            part = source[:, h * half_width : (h + 1) * half_width]
            total += jnp.dot(hot, part, preferred_element_type=jnp.float32)
        out_buf[b] = total.astype(jnp.bfloat16).reshape(shape6)

    def pick(b, where, h):
        ids = lax.broadcasted_iota(jnp.int32, (where.shape[0], slots), 1)
        hot = (ids == where + h * cap).astype(jnp.bfloat16)
        data = y_buf[b].reshape(slots, half_width)
        return jnp.dot(hot, data, preferred_element_type=jnp.float32)

    wait_peers = (
        len(greeted) + (line > 0).astype(jnp.int32) + (line < nl - 1).astype(jnp.int32)
    )
    cut = nx // 2

    def z_copy(b, n):
        src, dst, peer = (
            lambda: (out_buf.at[b, 2, :cut], relay.at[b, 0], right),
            lambda: (out_buf.at[b, 2, cut:], relay.at[b, 1], left),
            lambda: (out_buf.at[b, 1], z_buf.at[b, 0], right),
            lambda: (out_buf.at[b, 3], z_buf.at[b, 2], left),
            lambda: (relay.at[b, 0], z_buf.at[b, 1, :cut], right),
            lambda: (relay.at[b, 1], z_buf.at[b, 1, cut:], left),
        )[n]()
        return remote(src, dst, z_send.at[b, n], z_recv.at[b, n], peer)

    def x_copy(b, d, e):
        src = out_buf.at[b, 0, e] if d == 0 else z_buf.at[b, d - 1, e]
        dst = x_buf.at[b, d, e]
        if e == 0:
            return pltpu.make_async_copy(src, dst, x_recv.at[b, d, 0])
        return remote(src, dst, x_send.at[b, d, e], x_recv.at[b, d, e], x_peer[e])

    def y_copy(b, d, f):
        src, dst = x_buf.at[b, d, :, f], y_buf.at[b, d, :, f]
        if f == 0:
            return pltpu.make_async_copy(src, dst, y_recv.at[b, d, 0])
        return remote(src, dst, y_send.at[b, d, f], y_recv.at[b, d, f], y_peer[f])

    def z_start(names):
        if nz > 1:
            for b, n in names:
                z_copy(b, n).start()

    def z_forward(b):
        if nz > 1:
            for n in (0, 1):
                z_copy(b, n).wait_recv()
                z_copy(b, n + 4).start()

    def z_arrive(b, d):
        for n in {1: (2,), 2: (4, 5), 3: (3,)}[d]:
            z_copy(b, n).wait_recv()

    def x_start(b, d):
        for e in list(range(1, nx)) + [0]:
            x_copy(b, d, e).start()

    def y_start(b, d):
        x_copy(b, d, 0).wait()
        for e in range(1, nx):
            x_copy(b, d, e).wait_recv()
        for f in list(range(1, ny)) + [0]:
            y_copy(b, d, f).start()

    def y_arrive(b, d):
        y_copy(b, d, 0).wait()
        for f in range(1, ny):
            y_copy(b, d, f).wait_recv()

    w_copy = remote(w, w_far, w_send, w_recv, mate)
    tok_out = position(tok_slot[...], 1)
    loads[0].wait()
    place(0, cot, tok_out)
    pl.semaphore_wait(barrier, wait_peers)
    z_start([(0, n) for n in range(4)])
    x_start(0, 0)
    loads[1].wait()
    w_copy.start()
    loads[2].wait()
    merged[...] = jnp.zeros_like(merged)
    deep = 4 * piece

    def forward(i, carry):
        cols = pl.ds(pl.multiple_of(i * deep, deep), deep)
        hidden = gelu_value(pre[:, cols].astype(jnp.float32)).astype(jnp.bfloat16)
        merged[...] += jnp.dot(hidden, w[cols, :], preferred_element_type=jnp.float32)
        return carry

    lax.fori_loop(0, depth // deep, forward, 0)
    place(
        1,
        (merged[...] + bias[...].astype(jnp.float32)).astype(jnp.bfloat16),
        position(row_slot[...], 1),
    )
    y_start(0, 0)
    z_forward(0)
    z_start([(1, 0), (1, 1)])
    z_start([(1, 2), (1, 3)])
    x_start(1, 0)
    row_in = upright(position(row_slot[...], -1))
    tok_in = upright(position(tok_slot[...], -1))
    y_start(1, 0)
    if nz > 1:
        for d in (1, 3):
            z_arrive(0, d)
            x_start(0, d)
        for d in (1, 3):
            y_start(0, d)
        z_arrive(0, 2)
        x_start(0, 2)
        y_start(0, 2)
    for d in range(nz):
        y_arrive(0, d)

    for h in range(2):
        rows_full[:, h * half_width : (h + 1) * half_width] = pick(0, row_in, h).astype(
            jnp.bfloat16
        )
    mine = pl.ds(pl.multiple_of(core * half_rows, half_rows), half_rows)
    other = pl.ds(pl.multiple_of((1 - core) * half_rows, half_rows), half_rows)
    g_copy = remote(rows_full.at[other], rows_far, g_send, g_recv, mate)
    g_copy.start()
    z_forward(1)
    w_copy.wait_recv()
    g_copy.wait_recv()

    def columns(i):
        return pl.ds(pl.multiple_of(i * piece, piece), piece)

    def flow_copy(i, side, peer):
        return remote(
            flow_out.at[i], flow_in.at[side, i], flow_send.at[i], flow_recv.at[side, i], peer
        )

    def fin_copy(i, side, peer):
        block = grad.at[mine, columns(i)]
        return remote(block, block, fin_send.at[side, i], fin_recv.at[i], peer)

    def mate_copy(i):
        block = grad.at[mine, columns(i)]
        return remote(block, block, mate_send.at[i], mate_recv.at[i], mate)

    def mate_block(i):
        block = grad.at[other, columns(i)]
        return remote(block, block, mate_send.at[i], mate_recv.at[i], mate)

    def publish(i):
        @pl.when(has_low)
        def _():
            fin_copy(i, 0, down).start()

        @pl.when(has_high)
        def _():
            fin_copy(i, 1, up).start()

        mate_copy(i).start()

    away = jnp.where(line < middle, middle - line, line - middle)
    lag = 1 + LAG * away
    steps = count + 1 + LAG * (nl // 2 + (1 if nl > 1 else 0))

    def step(i, carry):
        @pl.when(i < count)
        def _():
            acc[...] = nt_dot(rows_full[mine, :], w[columns(i), :]) + nt_dot(
                rows_far[...], w_far[columns(i), :]
            )

            @pl.when(has_low)
            def _():
                flow_copy(i, 0, up).wait_recv()
                acc[...] += flow_in[0, i].astype(jnp.float32)

            @pl.when(has_high)
            def _():
                flow_copy(i, 1, down).wait_recv()
                acc[...] += flow_in[1, i].astype(jnp.float32)

            @pl.when(line != middle)
            def _():
                flow_out[i] = acc[...].astype(jnp.bfloat16)

            @pl.when(line < middle)
            def _():
                flow_copy(i, 0, up).start()

            @pl.when(line > middle)
            def _():
                flow_copy(i, 1, down).start()

            @pl.when(line == middle)
            def _():
                slope = gelu_slope(pre[mine, columns(i)].astype(jnp.float32))
                grad[mine, columns(i)] = (acc[...] * slope).astype(jnp.bfloat16)
                publish(i)

        j = i - lag

        @pl.when(jnp.logical_and(line != middle, jnp.logical_and(j >= 0, j < count)))
        def _():
            fin_copy(j, 0, down).wait_recv()
            publish(j)

        return carry

    first, second = count // 2, count // 2 + 6
    lax.fori_loop(0, first, step, 0)
    if nz > 1:
        for d in (1, 3, 2):
            z_arrive(1, d)
            x_start(1, d)
    lax.fori_loop(first, second, step, 0)
    if nz > 1:
        for d in (1, 3, 2):
            y_start(1, d)
    lax.fori_loop(second, steps, step, 0)

    loads[3].wait()
    for d in range(nz):
        y_arrive(1, d)
    for h in range(2):
        part = pl.ds(h * half_width, half_width)
        emb[:, part] = jnp.where(
            tok_in >= 0, pick(1, tok_in, h).astype(jnp.bfloat16), text[:, part]
        )

    emb_store = pltpu.make_async_copy(emb, emb_hbm, store_sem.at[0])
    emb_store.start()

    def drain(i, carry):
        @pl.when(line < middle)
        def _():
            flow_copy(i, 0, up).wait_send()

        @pl.when(line > middle)
        def _():
            flow_copy(i, 1, down).wait_send()

        @pl.when(has_low)
        def _():
            fin_copy(i, 0, down).wait_send()

        @pl.when(has_high)
        def _():
            fin_copy(i, 1, up).wait_send()

        mate_copy(i).wait_send()
        mate_block(i).wait_recv()
        return carry

    groups = 4
    span = count // groups
    stores = []
    for n in range(groups):
        lax.fori_loop(n * span, (n + 1) * span, drain, 0)
        cols = pl.ds(n * span * piece, span * piece)
        store = pltpu.make_async_copy(grad.at[:, cols], grad_hbm.at[:, cols], store_sem.at[n + 1])
        store.start()
        stores.append(store)
    w_copy.wait_send()
    g_copy.wait_send()
    if nz > 1:
        for b in range(2):
            for n in range(6):
                z_copy(b, n).wait_send()
    for b in range(2):
        for d in range(nz):
            for e in range(1, nx):
                x_copy(b, d, e).wait_send()
            for f in range(1, ny):
                y_copy(b, d, f).wait_send()
    emb_store.wait()
    for store in stores:
        store.wait()


def shards(cap, pre_act, w_out, b_out, row_slot, ctx_slot, text_rows, cotangent):
    nx, nz, ny, nl = (lax.axis_size(a) for a in ("x", "zh", "y", "zl"))
    rows, depth = pre_act.shape
    tokens, width = cotangent.shape
    half_width, half_rows = width // 2, rows // 2
    piece = depth // CHUNKS
    block = (nx, ny, 2 * cap, half_width)
    dma = pltpu.SemaphoreType.DMA
    bf16 = jnp.bfloat16
    scratch = [
        pltpu.VMEM((tokens, width), bf16),
        pltpu.VMEM((tokens, width), bf16),
        pltpu.VMEM((depth, width), bf16),
        pltpu.VMEM((rows, depth), bf16),
        pltpu.VMEM((rows, width), jnp.float32),
        pltpu.VMEM((tokens, width), bf16),
        pltpu.VMEM((rows, depth), bf16),
        dma((4,)), dma((5,)),
        pltpu.VMEM((2, nz, *block), bf16),
        pltpu.VMEM((2, max(nz - 1, 1), *block), bf16),
        pltpu.VMEM((2, 2, max(nx // 2, 1), *block[1:]), bf16),
        pltpu.VMEM((2, nz, *block), bf16),
        pltpu.VMEM((2, nz, *block), bf16),
        pltpu.VMEM((depth, width), bf16),
        pltpu.VMEM((rows, width), bf16),
        pltpu.VMEM((half_rows, width), bf16),
        pltpu.VMEM((2, CHUNKS, half_rows, piece), bf16),
        pltpu.VMEM((CHUNKS, half_rows, piece), bf16),
        pltpu.VMEM((half_rows, piece), jnp.float32),
        dma((2, 6)), dma((2, 6)),
        dma((2, nz, nx)), dma((2, nz, nx)),
        dma((2, nz, ny)), dma((2, nz, ny)),
        dma, dma, dma, dma,
        dma((CHUNKS,)), dma((2, CHUNKS)),
        dma((2, CHUNKS)), dma((CHUNKS,)),
        dma((CHUNKS,)), dma((CHUNKS,)),
    ]
    return pl.pallas_call(
        functools.partial(kernel, (nz, nx, ny, nl), cap),
        out_shape=(
            jax.ShapeDtypeStruct((tokens, width), bf16),
            jax.ShapeDtypeStruct((rows, depth), bf16),
        ),
        in_specs=[pl.BlockSpec(memory_space=pl.ANY)] * 4
        + [pl.BlockSpec(memory_space=pltpu.VMEM)] * 3,
        out_specs=(pl.BlockSpec(memory_space=pl.ANY),) * 2,
        scratch_shapes=scratch,
        compiler_params=pltpu.CompilerParams(
            collective_id=0, has_side_effects=True, vmem_limit_bytes=60 << 20
        ),
    )(
        cotangent, text_rows, w_out, pre_act,
        b_out.reshape(1, width), row_slot.reshape(1, rows), ctx_slot.reshape(1, tokens),
    )


def build(mesh, nx, nz, nl, cap):
    split = Mesh(
        mesh.devices.reshape(nx, nz, nl, 2, mesh.shape["grp"]), ("x", "zh", "zl", "core", "y")
    )
    ctx, tp = ("x", "zh", "y"), ("zl", "core")
    return jax.shard_map(
        functools.partial(shards, cap),
        mesh=split,
        in_specs=(P(ctx, None), P(None, tp), P(tp), P(ctx), P(ctx), P(ctx, tp), P(ctx, tp)),
        out_specs=(P(ctx, tp), P(ctx, None)),
        check_vma=False,
    )


def solution(mesh):
    return build(mesh, 4, mesh.shape["ctx"] // 4, mesh.shape["tp"] // 2, 8)
```
